32 devices in a mesh: groups: 2 (over y), tile: 4 (over z), sect: 4 (over x, core).
Axes of the slice: x: 2, y: 2, z: 4, core: 2. Of those that a mesh axis runs over, the one named last changes fastest.
Arguments:
- labels: int32 [16, 128, 512], P(('groups', 'sect'), None, 'tile'), parts along dimension 0, may hold values from 0 to 15
- classes: int32 [16, 128, 512], P(('groups', 'sect'), None, 'tile'), parts along dimension 0, may hold values from 0 to 7
- positions: int32 [8], P('groups'), parts along dimension 0, may hold values from 0 to 127
- phase_table: float32 [8], replicated, may hold values from -3.140625 to 3.140625
- brightness: float32 [16], replicated, may hold values from 0.2 to 2
- prop_taps: float32 [2, 2, 129], replicated, may hold values from -1 to 1, as said below
- detect_taps: float32 [2, 129], replicated, may hold values from 0 to 1, as said below
Outputs:
- image: float32 [16, 128, 512], P(('groups', 'sect'), None, 'tile'), parts along dimension 0
The draws below stay inside these ranges and needn't reach their ends.
There are 2 independent parts, one for each index of `groups`. The reference program is written for one: setup_inputs(seed, part) draws one part's arguments, and reference() takes and returns one part's arrays. A program takes and returns all parts, laid end to end along the dimension named above; an argument that names none is the same for every part. Nothing has to cross between parts.
Inputs may be any that keep to these rules, and one draw needn't show every extreme that they name: `prop_taps`: the squares of the 2 x 129 entries of each axis's propagation taps sum to 1. `detect_taps`: each axis's detection taps are positive and sum to 1.
All inputs are finite; a program needn't handle non-finite values.
Results may differ from the reference program's by a relative error of at most 0.0001.
Values sent between devices are 32-bit elements; how exact they have to be, the bound alone decides.
A program may use at most 64 MiB of HBM per device.

```python
import math
import jax
import jax.numpy as jnp
from jax import lax

TAPS = 129
RCLASS = 8
LABELS = 16
NY = 128
CZ = 128
POSITIONS = 4
NX = 8
NZ = 512


def draw_prop_taps(key, part):
    raw = jax.random.normal(key, (2, 2, TAPS), jnp.float32)
    scale = jnp.sqrt(jnp.sum(raw * raw, axis=(1, 2), keepdims=True))
    return raw / scale


def draw_detect_taps(key, part):
    raw = jax.random.uniform(key, (2, TAPS), jnp.float32, 0.1, 1.0)
    middle = (lax.broadcasted_iota(jnp.int32, (2, TAPS), 1) == TAPS // 2).astype(jnp.float32)
    raw = raw + middle * jnp.sum(raw, axis=1, keepdims=True)
    return raw / jnp.sum(raw, axis=1, keepdims=True)


def with_ends(entries, key, smallest, high):
    longest = entries.shape.index(max(entries.shape))
    spots = []
    for shift in (0, 1):
        where = [jax.random.randint(jax.random.fold_in(key, axis), (), 0, length) for axis, length in enumerate(entries.shape)]
        where[longest] = (where[longest] + shift) % entries.shape[longest]
        spots.append(tuple(where))
    return entries.at[spots[0]].set(smallest).at[spots[1]].set(high)


def setup_inputs(seed: int = 0, part: int = 0) -> dict:
    key_of = jax.random.split(jax.random.key(seed), 8)
    own_keys = jax.random.split(jax.random.fold_in(key_of[7], part), 8)
    return {
        "labels": with_ends(jax.random.randint(own_keys[0], (NX, NY, NZ), 0, LABELS), jax.random.fold_in(own_keys[0], 1), 0, LABELS - 1).astype(jnp.int32),
        "classes": with_ends(jax.random.randint(own_keys[1], (NX, NY, NZ), 0, RCLASS), jax.random.fold_in(own_keys[1], 1), 0, RCLASS - 1).astype(jnp.int32),
        "positions": with_ends(jax.random.randint(own_keys[2], (POSITIONS,), 0, NY), jax.random.fold_in(own_keys[2], 1), 0, NY - 1).astype(jnp.int32),
        "phase_table": jnp.clip(jax.random.uniform(key_of[3], (RCLASS,), jnp.float32, -3.140625, 3.140625), -3.140625, 3.140625),
        "brightness": jnp.clip(jnp.exp(jax.random.uniform(key_of[4], (LABELS,), jnp.float32, math.log(0.2), math.log(2.0))), 0.2, 2.0),
        "prop_taps": draw_prop_taps(jax.random.fold_in(key_of[7], 71), part),
        "detect_taps": draw_detect_taps(jax.random.fold_in(key_of[7], 71), part),
    }


SHEET_WIDTH = 6.0
AMPLITUDE = 2.0


def toeplitz(tap_rows, size_in, size_out, shift, period):
    count = tap_rows.shape[-1]
    inner = lax.broadcasted_iota(jnp.int32, (size_in, size_out), 0)
    outer = lax.broadcasted_iota(jnp.int32, (size_in, size_out), 1)
    offset = inner - outer + shift
    if period > 0:
        tap_place = lax.broadcasted_iota(jnp.int32, (count, period), 0)
        target = lax.broadcasted_iota(jnp.int32, (count, period), 1)
        folding = (jnp.mod(tap_place, period) == target).astype(tap_rows.dtype)
        table = jnp.einsum("...t,tj->...j", tap_rows, folding, precision=lax.Precision.HIGHEST)
        index = jnp.mod(offset, period).astype(jnp.int32)
        return jnp.take(table, index, axis=-1)
    index = jnp.clip(offset, 0, count - 1).astype(jnp.int32)
    valid = (offset >= 0) & (offset < count)
    values = jnp.take(tap_rows, index, axis=-1)
    return jnp.where(valid, values, jnp.zeros_like(values))


def complex_block(parts):
    real_part, imag_part = parts[0], parts[1]
    return jnp.stack([jnp.stack([real_part, imag_part]), jnp.stack([-imag_part, real_part])])


def lookup(indices, table):
    total = jnp.zeros(indices.shape, jnp.float32)
    for entry in range(table.shape[0]):
        total = total + jnp.where(indices == entry, table[entry], 0.0)
    return total


def sheet_plane(position, y_cells, z_cells):
    place = lax.broadcasted_iota(jnp.int32, (y_cells, z_cells), 0).astype(jnp.float32)
    offset = (place - position.astype(jnp.float32)) / SHEET_WIDTH
    real_part = AMPLITUDE * jnp.exp(-offset * offset)
    return jnp.stack([real_part, jnp.zeros_like(real_part)])


def apply_phase(field, cosine, sine):
    real_part = field[..., 0, :, :]
    imag_part = field[..., 1, :, :]
    return jnp.stack([real_part * cosine - imag_part * sine, real_part * sine + imag_part * cosine], axis=-3)


def along_y(field, y_band):
    return jnp.einsum("cdio,...ciz->...doz", y_band, field, precision=lax.Precision.HIGHEST, preferred_element_type=jnp.float32)


def windows_of(field, block, half_taps):
    z_cells = field.shape[-1]
    widths = [(0, 0)] * (field.ndim - 1) + [(half_taps, half_taps)]
    padded = jnp.pad(field, widths)
    pieces = [padded[..., number * block: number * block + block + 2 * half_taps] for number in range(z_cells // block)]
    return jnp.stack(pieces, axis=-2)


def reference(labels, classes, positions, phase_table, brightness, prop_taps, detect_taps):
    x_cells, y_cells, z_cells = labels.shape
    half_taps = prop_taps.shape[-1] // 2
    cosine = lookup(classes, jnp.cos(phase_table))
    sine = lookup(classes, jnp.sin(phase_table))
    y_band = complex_block(toeplitz(prop_taps[0], y_cells, y_cells, half_taps, y_cells))
    z_band = complex_block(toeplitz(prop_taps[1], CZ + 2 * half_taps, CZ, 0, 0))

    def advance(field, maps):
        field = apply_phase(field, maps[0], maps[1])
        field = along_y(field, y_band)
        windows = windows_of(field, CZ, half_taps)
        field = jnp.einsum("cybi,cdio->dybo", windows, z_band, precision=lax.Precision.HIGHEST, preferred_element_type=jnp.float32)
        field = field.reshape(2, y_cells, z_cells)
        return field, field[0] * field[0] + field[1] * field[1]

    collected = jnp.zeros(labels.shape, jnp.float32)
    for number in range(POSITIONS):
        start = sheet_plane(positions[number], y_cells, z_cells)
        _, left_power = lax.scan(advance, start, (cosine, sine))
        _, right_power = lax.scan(advance, start, (cosine, sine), reverse=True)
        collected = collected + left_power + right_power
    excitation = lookup(labels, brightness) * collected
    blur_y = toeplitz(detect_taps[0], y_cells, y_cells, half_taps, y_cells)
    blurred = jnp.einsum("io,xiz->xoz", blur_y, excitation, precision=lax.Precision.HIGHEST, preferred_element_type=jnp.float32)
    blur_z = toeplitz(detect_taps[1], CZ + 2 * half_taps, CZ, 0, 0)
    windows = windows_of(blurred, CZ, half_taps)
    image = jnp.einsum("xybi,io->xybo", windows, blur_z, precision=lax.Precision.HIGHEST, preferred_element_type=jnp.float32)
    return image.reshape(x_cells, y_cells, z_cells)
```

```python
import functools
import jax
import jax.numpy as jnp
from jax import lax
from jax.experimental import pallas as pl
from jax.experimental.pallas import tpu as pltpu
from jax.sharding import PartitionSpec as P

SHEET_WIDTH = 6.0
AMPLITUDE = 2.0
F32 = jnp.float32
BF16 = jnp.bfloat16


def padded_2(x, sides, width):
    for axis, dim in sides:
        count, length = (lax.axis_size(axis), x.shape[dim])
        up = [(i, (i + 1) % count) for i in range(count - 1)]
        down = [(j, i) for i, j in up]
        last = lax.slice_in_dim(x, length - width, length, axis=dim)
        first = lax.slice_in_dim(x, 0, width, axis=dim)
        before = lax.ppermute(last, axis, up)
        after = lax.ppermute(first, axis, down)
        x = jnp.concatenate([before, x, after], axis=dim)
    return x


def lookup(indices, table):
    total = jnp.zeros(indices.shape, jnp.float32)
    for entry in range(table.shape[0]):
        total = total + jnp.where(indices == entry, table[entry], 0.0)
    return total


def split(x):
    high = x.astype(BF16)
    return high, (x - high.astype(F32)).astype(BF16)


def roll_rows(row, size, shift):
    return pltpu.roll(jnp.broadcast_to(row, (size, size)), shift, 1, stride=1, stride_axis=0)


def circulant(row, size, half):
    folded = row[:, :size] + row[:, size:]
    return roll_rows(folded, size, half % size)


def windows(row, size):
    rolled = roll_rows(row[:, :size], size, 0)
    outer = lax.broadcasted_iota(jnp.int32, (size, size), 0)
    inner = lax.broadcasted_iota(jnp.int32, (size, size), 1)
    last = jnp.broadcast_to(row[:, size:size + 1], (size, size))
    first = jnp.where(inner >= outer, rolled, 0.0)
    second = jnp.where(inner < outer, rolled, jnp.where(inner == outer, last, 0.0))
    return first.T, second.T


def select_tree(bits, values):
    while len(values) > 1:
        bit, bits = bits[0], bits[1:]
        values = [jnp.where(bit, values[i + 1], values[i]) for i in range(0, len(values), 2)]
    return values[0]


def bit_masks(indices, count):
    masks, step = [], 1
    while step < count:
        masks.append((indices & step) != 0)
        step *= 2
    return masks


def entries(row, count, shape):
    return [jnp.broadcast_to(row[:, k:k + 1], shape) for k in range(count)]


def kernel(tiles, cls_ref, pos_ref, phase_ref, prop_ref, detect_ref, out_ref, blur_y_ref, blur_z_ref,
           taps, trig, y_band, z_band, field, rolled, high, low):
    x_cells, size = out_ref.shape[0], out_ref.shape[1]
    own_x = cls_ref.shape[2]
    count = prop_ref.shape[-1]
    half = count // 2
    section, sections = lax.axis_index("sect"), lax.axis_size("sect")
    own_tile = lax.axis_index("tile")
    per_side = sections // 2
    beams = 2 * pos_ref.shape[0] // sections
    left = section < per_side

    taps[...] = jnp.zeros_like(taps)
    for axis in range(2):
        for part in range(2):
            n = 2 * axis + part
            taps[n:n + 1, 0:count] = prop_ref[axis, part:part + 1, :]
        taps[4 + axis:5 + axis, 0:count] = detect_ref[axis:axis + 1, :]

    y_re, y_im = (circulant(taps[n:n + 1, :], size, half) for n in (0, 1))
    y_all = jnp.concatenate([jnp.concatenate([y_re, -y_im], 1), jnp.concatenate([y_im, y_re], 1)], 0)
    y_high, y_low = split(y_all)
    y_band[...] = jnp.concatenate([y_high, y_low, y_high], 1)
    z_re, z_im = windows(taps[2:3, :], size), windows(taps[3:4, :], size)
    parts = []
    for side in range(2):
        top = jnp.concatenate([z_re[side], z_im[side]], 1)
        bottom = jnp.concatenate([-z_im[side], z_re[side]], 1)
        parts.append(split(jnp.concatenate([top, bottom], 0)))
    z_band[...] = jnp.concatenate([p[0] for p in parts] * 2 + [p[1] for p in parts], 0)
    blur_y_ref[...] = circulant(taps[4:5, :], size, half)
    b0, b1 = windows(taps[5:6, :], size)
    blur_z_ref[...] = jnp.concatenate([b0, b1], 0)

    classes = phase_ref.shape[1]
    trig[0:1, 0:classes] = jnp.cos(phase_ref[...])
    trig[1:2, 0:classes] = jnp.sin(phase_ref[...])
    place = lax.broadcasted_iota(jnp.int32, (size, size), 0).astype(F32)
    for b in range(beams):
        index = (section % per_side) * beams + b
        offset = (place - pos_ref[index].astype(F32)) / SHEET_WIDTH
        start = AMPLITUDE * jnp.exp(-offset * offset)

        @pl.loop(0, tiles)
        def _(j):
            field[j, b * size:(b + 1) * size, 0:size] = start
            field[j, b * size:(b + 1) * size, size:] = jnp.zeros_like(start)

    lane = lax.broadcasted_iota(jnp.int32, (size, size), 1)
    upper = lane < (size - half)
    unroll = tiles if tiles <= 4 else 1

    def shifted(j, before, now):
        joined = jnp.where(jnp.concatenate([jnp.concatenate([upper] * 2, 1)] * beams, 0), before, now)
        high[j], low[j] = split(joined)

    def slice_step(step, carry):
        x = jnp.where(left, step, x_cells - 1 - step)
        owner, inner = x // own_x, x % own_x
        cosines = entries(trig[0:1, :], classes, (size, size))
        sines = entries(trig[1:2, :], classes, (size, size))
        rolled[...] = jnp.zeros_like(rolled)

        def first(j, carry):
            masks = bit_masks(cls_ref[owner, j, inner], classes)
            cosine, sine = select_tree(masks, cosines), select_tree(masks, sines)
            reals, imags = [], []
            for b in range(beams):
                re = field[j, b * size:(b + 1) * size, 0:size]
                im = field[j, b * size:(b + 1) * size, size:]
                reals.append(re * cosine - im * sine)
                imags.append(re * sine + im * cosine)
            plane = jnp.concatenate([jnp.concatenate(reals, 1), jnp.concatenate(imags, 1)], 0)
            u_high, u_low = split(plane)
            v = jnp.dot(y_band[...], jnp.concatenate([u_high, u_high, u_low], 0), preferred_element_type=F32)
            rows = []
            for b in range(beams):
                cols = [pltpu.roll(v[c * size:(c + 1) * size, b * size:(b + 1) * size], half, 1) for c in range(2)]
                rows.append(jnp.concatenate(cols, 1))
            now = jnp.concatenate(rows, 0)
            shifted(j, rolled[...], now)
            rolled[...] = now
            return carry

        lax.fori_loop(0, tiles, first, 0, unroll=unroll)
        shifted(tiles, rolled[...], jnp.zeros_like(rolled))

        def second(j, carry):
            sides = [high[j], high[j + 1], low[j], low[j + 1], high[j], high[j + 1]]
            field[j] = jnp.dot(jnp.concatenate(sides, 1), z_band[...], preferred_element_type=F32)
            return carry

        lax.fori_loop(0, tiles, second, 0, unroll=unroll)
        w = field[own_tile]
        energy = w * w
        energy = energy[:, :size] + energy[:, size:]
        total = energy[0:size]
        for b in range(1, beams):
            total = total + energy[b * size:(b + 1) * size]
        out_ref[x] = total
        return carry

    lax.fori_loop(0, x_cells, slice_step, 0)


def on_device(labels, classes, positions, phase_table, brightness, prop_taps, detect_taps):
    own_x, size, _ = labels.shape
    half_taps = prop_taps.shape[-1] // 2
    sections, tiles = lax.axis_size("sect"), lax.axis_size("tile")
    x_cells = own_x * sections
    beams = 2 * positions.shape[0] // sections
    every_class = lax.all_gather(lax.all_gather(classes, "tile"), "sect")
    vmem, smem = pl.BlockSpec(memory_space=pltpu.VMEM), pl.BlockSpec(memory_space=pltpu.SMEM)
    rows = beams * size
    totals, blur_y, blur_z = pl.pallas_call(
        functools.partial(kernel, tiles),
        out_shape=(
            jax.ShapeDtypeStruct((x_cells, size, size), F32),
            jax.ShapeDtypeStruct((size, size), F32),
            jax.ShapeDtypeStruct((2 * size, size), F32),
        ),
        in_specs=[vmem, smem, vmem, vmem, vmem],
        out_specs=(vmem, vmem, vmem),
        scratch_shapes=[
            pltpu.VMEM((8, 2 * size), F32),
            pltpu.VMEM((8, 128), F32),
            pltpu.VMEM((2 * size, 6 * size), BF16),
            pltpu.VMEM((12 * size, 2 * size), BF16),
            pltpu.VMEM((tiles, rows, 2 * size), F32),
            pltpu.VMEM((rows, 2 * size), F32),
            pltpu.VMEM((tiles + 1, rows, 2 * size), BF16),
            pltpu.VMEM((tiles + 1, rows, 2 * size), BF16),
        ],
        compiler_params=pltpu.CompilerParams(vmem_limit_bytes=58 * 1024 * 1024),
    )(every_class, positions, phase_table.reshape(1, -1), prop_taps, detect_taps)
    collected = lax.psum_scatter(totals, "sect", scatter_dimension=0, tiled=True)
    excitation = lookup(labels, brightness) * collected
    blurred = jnp.einsum("yi,xiz->xyz", blur_y, excitation, precision=lax.Precision.HIGHEST,
                         preferred_element_type=F32)
    padded = padded_2(blurred, (("tile", 2),), half_taps)
    return jnp.einsum("xyi,io->xyo", padded, blur_z, precision=lax.Precision.HIGHEST,
                      preferred_element_type=F32)


def solution(mesh):
    in_specs = (
        P(("groups", "sect"), None, "tile"),
        P(("groups", "sect"), None, "tile"),
        P("groups"),
        P(),
        P(),
        P(),
        P(),
    )
    out_specs = P(("groups", "sect"), None, "tile")
    return jax.shard_map(
        on_device, mesh=mesh, in_specs=in_specs, out_specs=out_specs, check_vma=False
    )
```

```python
import functools
import jax
import jax.numpy as jnp
from jax import lax
from jax.experimental import pallas as pl
from jax.experimental.pallas import tpu as pltpu
from jax.sharding import PartitionSpec as P

SHEET_WIDTH = 6.0
AMPLITUDE = 2.0
F32 = jnp.float32
BF16 = jnp.bfloat16
MESH = pl.DeviceIdType.MESH


def split(x):
    high = x.astype(BF16)
    return high, (x - high.astype(F32)).astype(BF16)


def roll_rows(row, size, shift):
    return pltpu.roll(jnp.broadcast_to(row, (size, size)), shift, 1, stride=1, stride_axis=0)


def circulant(row, size, half):
    folded = row[:, :size] + row[:, size:]
    return roll_rows(folded, size, half % size)


def windows(row, size):
    rolled = roll_rows(row[:, :size], size, 0)
    outer = lax.broadcasted_iota(jnp.int32, (size, size), 0)
    inner = lax.broadcasted_iota(jnp.int32, (size, size), 1)
    last = jnp.broadcast_to(row[:, size:size + 1], (size, size))
    first = jnp.where(inner >= outer, rolled, 0.0)
    second = jnp.where(inner < outer, rolled, jnp.where(inner == outer, last, 0.0))
    return first.T, second.T


def select_tree(bits, values):
    while len(values) > 1:
        bit, bits = bits[0], bits[1:]
        values = [jnp.where(bit, values[i + 1], values[i]) for i in range(0, len(values), 2)]
    return values[0]


def bit_masks(indices, count):
    masks, step = [], 1
    while step < count:
        masks.append((indices & step) != 0)
        step *= 2
    return masks


def entries(row, count, shape):
    return [jnp.broadcast_to(row[:, k:k + 1], shape) for k in range(count)]


def dot3(a, b):
    a_high, a_low = split(a)
    b_high, b_low = split(b)
    return jnp.dot(jnp.concatenate([a_high, a_low, a_high], 1), jnp.concatenate([b_high, b_high, b_low], 0),
                   preferred_element_type=F32)


def kernel(tiles, sections, labels_ref, classes_ref, pos_ref, phase_ref, bright_ref, prop_ref, detect_ref, out_ref,
           held, label_held, taps, y_band, z_band, field, rolled, high, low, energy, gathered, edges, edge_in,
           arrived, along, across, beside, label_sem, energy_out, energy_in, edge_out, edge_sem):
    own_x, size = out_ref.shape[0], out_ref.shape[1]
    x_cells = own_x * sections
    count = prop_ref.shape[-1]
    half = count // 2
    section, tile = lax.axis_index("sect"), lax.axis_index("tile")
    per_side = sections // 2
    beams = 2 * pos_ref.shape[0] // sections
    left = section < per_side
    place_in_side = section % per_side
    mirror = (section + per_side) % sections
    partners = [section - place_in_side + (place_in_side + m) % per_side for m in range(1, per_side)]

    def tile_at(d):
        return (tile + d) % tiles

    def section_at(d):
        return (section + d) % sections

    barrier = pltpu.get_barrier_semaphore()

    @pl.loop(1, tiles)
    def _(d):
        pl.semaphore_signal(barrier, inc=1, device_id={"tile": tile_at(d)}, device_id_type=MESH)

    for d in range(1, sections):
        pl.semaphore_signal(barrier, inc=1, device_id={"sect": section_at(d)}, device_id_type=MESH)
    pl.semaphore_wait(barrier, tiles - 1 + sections - 1)

    def own_copy(inner):
        return pltpu.make_async_copy(
            classes_ref.at[inner], held.at[section, inner, tile], arrived.at[section, inner, tile])

    def slab_copy(source, owner, inner, j, sem, device):
        return pltpu.make_async_remote_copy(
            src_ref=source, dst_ref=held.at[owner, inner, j], send_sem=sem,
            recv_sem=arrived.at[owner, inner, j], device_id=device, device_id_type=MESH)

    def along_copy(inner, d):
        return slab_copy(classes_ref.at[inner], section, inner, tile, along.at[inner, d], {"tile": tile_at(d)})

    def mirror_copy(inner, j, source):
        return slab_copy(source, section, inner, j, across.at[inner, j], {"sect": mirror})

    def partner_copies(owner, kind, inner, j, source):
        return [slab_copy(source, owner, inner, j, beside.at[kind, m, inner, j], {"sect": other})
                for m, other in enumerate(partners)]

    def await_slab(owner, inner, j):
        slab_copy(held.at[owner, inner, j], owner, inner, j, across.at[inner, j], {"sect": mirror}).wait_recv()

    def own_inner(n):
        return jnp.where(left, n, own_x - 1 - n)

    def mirror_inner(n):
        return jnp.where(left, own_x - 1 - n, n)

    for n in range(own_x):
        inner = own_inner(n)
        own_copy(inner).start()

        @pl.loop(1, tiles)
        def _(d):
            along_copy(inner, d).start()

        for copy in partner_copies(section, 0, inner, tile, classes_ref.at[inner]):
            copy.start()
        mirror_copy(inner, tile, classes_ref.at[inner]).start()
    label_copy = pltpu.make_async_copy(labels_ref, label_held, label_sem)
    label_copy.start()

    def serve_own(n):
        inner = own_inner(n)
        own_copy(inner).wait()

        @pl.loop(1, tiles)
        def _(d):
            j = tile_at(d)
            await_slab(section, inner, j)
            for copy in partner_copies(section, 0, inner, j, held.at[section, inner, j]):
                copy.start()
            mirror_copy(inner, j, held.at[section, inner, j]).start()

    def serve_mirror(n):
        inner = mirror_inner(n)

        @pl.loop(0, tiles)
        def _(j):
            await_slab(mirror, inner, j)
            for copy in partner_copies(mirror, 1, inner, j, held.at[mirror, inner, j]):
                copy.start()

    def energy_copy(x):
        inner = x % own_x
        return pltpu.make_async_remote_copy(
            src_ref=energy.at[x], dst_ref=gathered.at[section, inner], send_sem=energy_out.at[x],
            recv_sem=energy_in.at[section, inner], device_id={"sect": x // own_x}, device_id_type=MESH)

    taps[...] = jnp.zeros_like(taps)
    for axis in range(2):
        for part in range(2):
            n = 2 * axis + part
            taps[n:n + 1, 0:count] = prop_ref[axis, part:part + 1, :]
        taps[4 + axis:5 + axis, 0:count] = detect_ref[axis:axis + 1, :]

    y_re, y_im = (circulant(taps[n:n + 1, :], size, half) for n in (0, 1))
    y_all = jnp.concatenate([jnp.concatenate([y_re, -y_im], 1), jnp.concatenate([y_im, y_re], 1)], 0)
    y_high, y_low = split(y_all)
    y_band[...] = jnp.concatenate([y_high, y_low, y_high], 1)
    z_re, z_im = windows(taps[2:3, :], size), windows(taps[3:4, :], size)
    parts = []
    for side in range(2):
        top = jnp.concatenate([z_re[side], z_im[side]], 1)
        bottom = jnp.concatenate([-z_im[side], z_re[side]], 1)
        parts.append(split(jnp.concatenate([top, bottom], 0)))
    z_band[...] = jnp.concatenate([p[0] for p in parts] * 2 + [p[1] for p in parts], 0)

    classes = phase_ref.shape[0]
    spot = lax.broadcasted_iota(jnp.int32, (8, 128), 1)
    phases = jnp.zeros((8, 128), F32)
    for k in range(classes):
        phases = jnp.where(spot == k, phase_ref[k], phases)
    cos_row, sin_row = jnp.cos(phases)[0:1], jnp.sin(phases)[0:1]
    place = lax.broadcasted_iota(jnp.int32, (size, size), 0).astype(F32)
    for b in range(beams):
        index = place_in_side * beams + b
        offset = (place - pos_ref[index].astype(F32)) / SHEET_WIDTH
        start = AMPLITUDE * jnp.exp(-offset * offset)

        @pl.loop(0, tiles)
        def _(j):
            field[j, b * size:(b + 1) * size, 0:size] = start
            field[j, b * size:(b + 1) * size, size:] = jnp.zeros_like(start)

    lane = lax.broadcasted_iota(jnp.int32, (size, size), 1)
    upper = lane < (size - half)
    unroll = tiles if tiles <= 4 else 1

    def shifted(j, before, now):
        joined = jnp.where(jnp.concatenate([jnp.concatenate([upper] * 2, 1)] * beams, 0), before, now)
        high[j], low[j] = split(joined)

    first_mirror = x_cells // 2 - own_x + 1

    def slice_step(step, carry):
        x = jnp.where(left, step, x_cells - 1 - step)
        owner, inner = x // own_x, x % own_x
        for n in range(own_x):
            pl.when(step == n)(functools.partial(serve_own, n))
            pl.when(step == first_mirror + n)(functools.partial(serve_mirror, n))

        @pl.when(owner % per_side != place_in_side)
        def _():
            @pl.loop(0, tiles)
            def _(j):
                await_slab(owner, inner, j)

        cosines = entries(cos_row, classes, (size, size))
        sines = entries(sin_row, classes, (size, size))
        rolled[...] = jnp.zeros_like(rolled)

        def first(j, carry):
            masks = bit_masks(held[owner, inner, j], classes)
            cosine, sine = select_tree(masks, cosines), select_tree(masks, sines)
            reals, imags = [], []
            for b in range(beams):
                re = field[j, b * size:(b + 1) * size, 0:size]
                im = field[j, b * size:(b + 1) * size, size:]
                reals.append(re * cosine - im * sine)
                imags.append(re * sine + im * cosine)
            plane = jnp.concatenate([jnp.concatenate(reals, 1), jnp.concatenate(imags, 1)], 0)
            u_high, u_low = split(plane)
            v = jnp.dot(y_band[...], jnp.concatenate([u_high, u_high, u_low], 0), preferred_element_type=F32)
            rows = []
            for b in range(beams):
                cols = [pltpu.roll(v[c * size:(c + 1) * size, b * size:(b + 1) * size], half, 1) for c in range(2)]
                rows.append(jnp.concatenate(cols, 1))
            now = jnp.concatenate(rows, 0)
            shifted(j, rolled[...], now)
            rolled[...] = now
            return carry

        lax.fori_loop(0, tiles, first, 0, unroll=unroll)
        shifted(tiles, rolled[...], jnp.zeros_like(rolled))

        def second(j, carry):
            sides = [high[j], high[j + 1], low[j], low[j + 1], high[j], high[j + 1]]
            field[j] = jnp.dot(jnp.concatenate(sides, 1), z_band[...], preferred_element_type=F32)
            return carry

        lax.fori_loop(0, tiles, second, 0, unroll=unroll)
        w = field[tile]
        power = w * w
        power = power[:, :size] + power[:, size:]
        total = power[0:size]
        for b in range(1, beams):
            total = total + power[b * size:(b + 1) * size]
        energy[x] = total
        pl.when(owner != section)(lambda: energy_copy(x).start())
        return carry

    lax.fori_loop(0, x_cells, slice_step, 0)

    blur_y = circulant(taps[4:5, :], size, half)
    blur_z = jnp.concatenate(windows(taps[5:6, :], size), 0)
    label_copy.wait()
    lit = []
    for inner in range(own_x):
        masks = bit_masks(label_held[inner], bright_ref.shape[0])
        lit.append(select_tree(masks, [jnp.full((size, size), bright_ref[k]) for k in range(bright_ref.shape[0])]))

    def received(other, inner):
        return pltpu.make_async_remote_copy(
            src_ref=energy.at[0], dst_ref=gathered.at[other, inner], send_sem=energy_out.at[0],
            recv_sem=energy_in.at[other, inner], device_id={"sect": other}, device_id_type=MESH)

    columns = []
    for inner in range(own_x):
        total = energy[section * own_x + inner]
        for d in range(1, sections):
            received(section_at(d), inner).wait_recv()
            total = total + gathered[section_at(d), inner]
        columns.append(lit[inner] * total)
    blurred = dot3(blur_y, jnp.concatenate(columns, 1))

    top = lax.broadcasted_iota(jnp.int32, (size // 2, size), 1) < half
    turned = []
    for inner in range(own_x):
        block = blurred[:, inner * size:(inner + 1) * size]
        turn = pltpu.roll(block, half, 1)
        turned.append(turn)
        edges[0, inner] = jnp.where(top, turn[:size // 2], block[size // 2:])
        edges[1, inner] = jnp.where(top, block[:size // 2], turn[size // 2:])

    def edge_copy(way):
        return pltpu.make_async_remote_copy(
            src_ref=edges.at[way], dst_ref=edge_in.at[way], send_sem=edge_out.at[way],
            recv_sem=edge_sem.at[way], device_id={"tile": tile_at(1 if way == 0 else tiles - 1)},
            device_id_type=MESH)

    has_next, has_before = tile < tiles - 1, tile > 0
    edge_in_ok = (has_before, has_next)
    edge_out_ok = (has_next, has_before)
    for way in range(2):
        pl.when(edge_out_ok[way])(lambda: edge_copy(way).start())
    for way in range(2):
        @pl.when(jnp.logical_not(edge_in_ok[way]))
        def _():
            edge_in[way] = jnp.zeros(edge_in.shape[1:], F32)

        pl.when(edge_in_ok[way])(lambda: edge_copy(way).wait_recv())

    planes = []
    for inner in range(own_x):
        turn = turned[inner]
        before, after = edge_in[0, inner], edge_in[1, inner]
        before = jnp.concatenate([before, pltpu.roll(before, half, 1)], 0)
        after = jnp.concatenate([pltpu.roll(after, half, 1), after], 0)
        planes.append(jnp.concatenate([jnp.where(upper, before, turn), jnp.where(upper, turn, after)], 1))
    image = dot3(jnp.concatenate(planes, 0), blur_z)
    for inner in range(own_x):
        out_ref[inner] = image[inner * size:(inner + 1) * size]

    for way in range(2):
        pl.when(edge_out_ok[way])(lambda: edge_copy(way).wait_send())

    @pl.loop(0, x_cells)
    def _(x):
        pl.when(x // own_x != section)(lambda: energy_copy(x).wait_send())

    for inner in range(own_x):
        @pl.loop(1, tiles)
        def _(d):
            along_copy(inner, d).wait_send()

        @pl.loop(0, tiles)
        def _(j):
            mirror_copy(inner, j, held.at[section, inner, j]).wait_send()
            for kind, owner in ((0, section), (1, mirror)):
                for copy in partner_copies(owner, kind, inner, j, held.at[owner, inner, j]):
                    copy.wait_send()


def on_device(labels, classes, positions, phase_table, brightness, prop_taps, detect_taps):
    own_x, size, _ = labels.shape
    sections, tiles = lax.axis_size("sect"), lax.axis_size("tile")
    x_cells = own_x * sections
    beams = 2 * positions.shape[0] // sections
    vmem, smem = pl.BlockSpec(memory_space=pltpu.VMEM), pl.BlockSpec(memory_space=pltpu.SMEM)
    anywhere = pl.BlockSpec(memory_space=pl.ANY)
    rows = beams * size
    dma = pltpu.SemaphoreType.DMA
    return pl.pallas_call(
        functools.partial(kernel, tiles, sections),
        out_shape=jax.ShapeDtypeStruct((own_x, size, size), F32),
        in_specs=[anywhere, anywhere, smem, smem, smem, vmem, vmem],
        out_specs=vmem,
        scratch_shapes=[
            pltpu.VMEM((sections, own_x, tiles, size, size), jnp.int32),
            pltpu.VMEM((own_x, size, size), jnp.int32),
            pltpu.VMEM((8, 2 * size), F32),
            pltpu.VMEM((2 * size, 6 * size), BF16),
            pltpu.VMEM((12 * size, 2 * size), BF16),
            pltpu.VMEM((tiles, rows, 2 * size), F32),
            pltpu.VMEM((rows, 2 * size), F32),
            pltpu.VMEM((tiles + 1, rows, 2 * size), BF16),
            pltpu.VMEM((tiles + 1, rows, 2 * size), BF16),
            pltpu.VMEM((x_cells, size, size), F32),
            pltpu.VMEM((sections, own_x, size, size), F32),
            pltpu.VMEM((2, own_x, size // 2, size), F32),
            pltpu.VMEM((2, own_x, size // 2, size), F32),
            dma((sections, own_x, tiles)),
            dma((own_x, tiles)),
            dma((own_x, tiles)),
            dma((2, max(sections // 2 - 1, 1), own_x, tiles)),
            dma,
            dma((x_cells,)),
            dma((sections, own_x)),
            dma((2,)),
            dma((2,)),
        ],
        compiler_params=pltpu.CompilerParams(
            vmem_limit_bytes=60 * 1024 * 1024, collective_id=0, has_side_effects=True),
    )(labels, classes, positions, phase_table, brightness, prop_taps, detect_taps)


def solution(mesh):
    in_specs = (
        P(("groups", "sect"), None, "tile"),
        P(("groups", "sect"), None, "tile"),
        P("groups"),
        P(),
        P(),
        P(),
        P(),
    )
    out_specs = P(("groups", "sect"), None, "tile")
    return jax.shard_map(
        on_device, mesh=mesh, in_specs=in_specs, out_specs=out_specs, check_vma=False
    )
```

```python
import functools
import jax
import jax.numpy as jnp
from jax import lax
from jax.experimental import pallas as pl
from jax.experimental.pallas import tpu as pltpu
from jax.sharding import PartitionSpec as P

SHEET_WIDTH = 6.0
AMPLITUDE = 2.0
F32 = jnp.float32
BF16 = jnp.bfloat16
MESH = pl.DeviceIdType.MESH


def split(x):
    high = x.astype(BF16)
    return high, (x - high.astype(F32)).astype(BF16)


def roll_rows(row, size, shift):
    return pltpu.roll(jnp.broadcast_to(row, (size, size)), shift, 1, stride=1, stride_axis=0)


def circulant(row, size, half):
    folded = row[:, :size] + row[:, size:]
    return roll_rows(folded, size, half % size)


def windows(row, size):
    rolled = roll_rows(row[:, :size], size, 0)
    outer = lax.broadcasted_iota(jnp.int32, (size, size), 0)
    inner = lax.broadcasted_iota(jnp.int32, (size, size), 1)
    last = jnp.broadcast_to(row[:, size:size + 1], (size, size))
    first = jnp.where(inner >= outer, rolled, 0.0)
    second = jnp.where(inner < outer, rolled, jnp.where(inner == outer, last, 0.0))
    return first.T, second.T


def select_tree(bits, values):
    while len(values) > 1:
        bit, bits = bits[0], bits[1:]
        values = [jnp.where(bit, values[i + 1], values[i]) for i in range(0, len(values), 2)]
    return values[0]


def bit_masks(indices, count):
    masks, step = [], 1
    while step < count:
        masks.append((indices & step) != 0)
        step *= 2
    return masks


def entries(row, count, shape):
    return [jnp.broadcast_to(row[:, k:k + 1], shape) for k in range(count)]


def dot3(a, b):
    a_high, a_low = split(a)
    b_high, b_low = split(b)
    return jnp.dot(jnp.concatenate([a_high, a_low, a_high], 1), jnp.concatenate([b_high, b_high, b_low], 0),
                   preferred_element_type=F32)


def kernel(tiles, sections, labels_ref, classes_ref, pos_ref, phase_ref, bright_ref, prop_ref, detect_ref, out_ref,
           held, label_held, taps, y_band, z_band, field, rolled, high, low, energy, gathered, edges, edge_in,
           arrived, along, relay, across, beside, label_sem, energy_out, energy_in, edge_out, edge_sem):
    own_x, size = out_ref.shape[0], out_ref.shape[1]
    x_cells = own_x * sections
    count = prop_ref.shape[-1]
    half = count // 2
    section, tile = lax.axis_index("sect"), lax.axis_index("tile")
    per_side = sections // 2
    beams = 2 * pos_ref.shape[0] // sections
    left = section < per_side
    place_in_side = section % per_side
    mirror = (section + per_side) % sections
    partners = [section - place_in_side + (place_in_side + m) % per_side for m in range(1, per_side)]

    def tile_at(d):
        return (tile + d) % tiles

    def section_at(d):
        return (section + d) % sections

    barrier = pltpu.get_barrier_semaphore()

    @pl.loop(1, tiles)
    def _(d):
        pl.semaphore_signal(barrier, inc=1, device_id={"tile": tile_at(d)}, device_id_type=MESH)

    for d in range(1, sections):
        pl.semaphore_signal(barrier, inc=1, device_id={"sect": section_at(d)}, device_id_type=MESH)
    pl.semaphore_wait(barrier, tiles - 1 + sections - 1)

    def own_copy(inner):
        return pltpu.make_async_copy(
            classes_ref.at[inner], held.at[section, inner, tile], arrived.at[section, inner, tile])

    def slab_copy(source, owner, inner, j, sem, device):
        return pltpu.make_async_remote_copy(
            src_ref=source, dst_ref=held.at[owner, inner, j], send_sem=sem,
            recv_sem=arrived.at[owner, inner, j], device_id=device, device_id_type=MESH)

    def along_copy(inner, d):
        return slab_copy(classes_ref.at[inner], section, inner, tile, along.at[inner, d], {"tile": tile_at(d)})

    def relay_copy(way, j, source):
        other = tile_at(1 if way == 0 else tiles - 1)
        return slab_copy(source, section, own_inner(0), j, relay.at[way, j], {"tile": other})

    def mirror_copy(inner, j, source):
        return slab_copy(source, section, inner, j, across.at[inner, j], {"sect": mirror})

    def partner_copies(owner, kind, inner, j, source):
        return [slab_copy(source, owner, inner, j, beside.at[kind, m, inner, j], {"sect": other})
                for m, other in enumerate(partners)]

    def await_slab(owner, inner, j):
        slab_copy(held.at[owner, inner, j], owner, inner, j, across.at[inner, j], {"sect": mirror}).wait_recv()

    first_left, first_right = place_in_side == 0, place_in_side == per_side - 1
    ascending = jnp.where(left, first_left, jnp.logical_not(first_right))
    mirror_ascending = jnp.where(left, jnp.logical_not(first_right), first_left)
    has_next, has_before = tile < tiles - 1, tile > 0

    def own_inner(n):
        return jnp.where(ascending, n, own_x - 1 - n)

    def mirror_inner(n):
        return jnp.where(mirror_ascending, n, own_x - 1 - n)

    for n in range(own_x):
        inner = own_inner(n)
        own_copy(inner).start()
        if n == 0:
            pl.when(has_next)(lambda: relay_copy(0, tile, classes_ref.at[inner]).start())
            pl.when(has_before)(lambda: relay_copy(1, tile, classes_ref.at[inner]).start())
        for copy in partner_copies(section, 0, inner, tile, classes_ref.at[inner]):
            copy.start()
        mirror_copy(inner, tile, classes_ref.at[inner]).start()
    label_copy = pltpu.make_async_copy(labels_ref, label_held, label_sem)
    label_copy.start()

    def send_along():
        for n in range(1, own_x):
            @pl.loop(1, tiles)
            def _(d):
                along_copy(own_inner(n), d).start()

    def serve_own(n):
        inner = own_inner(n)

        def arrival(j, way, onward):
            await_slab(section, inner, j)
            if n == 0:
                pl.when(onward)(lambda: relay_copy(way, j, held.at[section, inner, j]).start())
            for copy in partner_copies(section, 0, inner, j, held.at[section, inner, j]):
                copy.start()
            mirror_copy(inner, j, held.at[section, inner, j]).start()

        @pl.loop(1, tiles)
        def _(d):
            pl.when(tile - d >= 0)(lambda: arrival(tile - d, 0, has_next))
            pl.when(tile + d < tiles)(lambda: arrival(tile + d, 1, has_before))
            if n == 0:
                pl.when(d == 1)(send_along)

        own_copy(inner).wait()

    def serve_mirror(n):
        inner = mirror_inner(n)

        @pl.loop(0, tiles)
        def _(j):
            await_slab(mirror, inner, j)
            for copy in partner_copies(mirror, 1, inner, j, held.at[mirror, inner, j]):
                copy.start()

    def energy_copy(x):
        inner = x % own_x
        return pltpu.make_async_remote_copy(
            src_ref=energy.at[x], dst_ref=gathered.at[section, inner], send_sem=energy_out.at[x],
            recv_sem=energy_in.at[section, inner], device_id={"sect": x // own_x}, device_id_type=MESH)

    taps[...] = jnp.zeros_like(taps)
    for axis in range(2):
        for part in range(2):
            n = 2 * axis + part
            taps[n:n + 1, 0:count] = prop_ref[axis, part:part + 1, :]
        taps[4 + axis:5 + axis, 0:count] = detect_ref[axis:axis + 1, :]

    y_re, y_im = (circulant(taps[n:n + 1, :], size, half) for n in (0, 1))
    y_all = jnp.concatenate([jnp.concatenate([y_re, -y_im], 1), jnp.concatenate([y_im, y_re], 1)], 0)
    y_high, y_low = split(y_all)
    y_band[...] = jnp.concatenate([y_high, y_low, y_high], 1)
    z_re, z_im = windows(taps[2:3, :], size), windows(taps[3:4, :], size)
    parts = []
    for side in range(2):
        top = jnp.concatenate([z_re[side], z_im[side]], 1)
        bottom = jnp.concatenate([-z_im[side], z_re[side]], 1)
        parts.append(split(jnp.concatenate([top, bottom], 0)))
    z_band[...] = jnp.concatenate([p[0] for p in parts] * 2 + [p[1] for p in parts], 0)

    classes = phase_ref.shape[0]
    spot = lax.broadcasted_iota(jnp.int32, (8, 128), 1)
    phases = jnp.zeros((8, 128), F32)
    for k in range(classes):
        phases = jnp.where(spot == k, phase_ref[k], phases)
    cos_row, sin_row = jnp.cos(phases)[0:1], jnp.sin(phases)[0:1]
    place = lax.broadcasted_iota(jnp.int32, (size, size), 0).astype(F32)
    for b in range(beams):
        index = place_in_side * beams + b
        offset = (place - pos_ref[index].astype(F32)) / SHEET_WIDTH
        start = AMPLITUDE * jnp.exp(-offset * offset)

        @pl.loop(0, tiles)
        def _(j):
            field[j, b * size:(b + 1) * size, 0:size] = start
            field[j, b * size:(b + 1) * size, size:] = jnp.zeros_like(start)

    lane = lax.broadcasted_iota(jnp.int32, (size, size), 1)
    upper = lane < (size - half)
    unroll = tiles if tiles <= 4 else 1

    def shifted(j, before, now):
        joined = jnp.where(jnp.concatenate([jnp.concatenate([upper] * 2, 1)] * beams, 0), before, now)
        high[j], low[j] = split(joined)

    middle = x_cells // 2

    def slice_step(step, carry):
        x = jnp.where(left, step, x_cells - 1 - step)
        owner, inner = x // own_x, x % own_x
        for n in range(own_x):
            pl.when(step == n)(functools.partial(serve_own, n))
            pl.when(step == (middle - 1 if n == 0 else middle + n if per_side > 1 else middle))(functools.partial(serve_mirror, n))

        @pl.when(owner % per_side != place_in_side)
        def _():
            @pl.loop(0, tiles)
            def _(j):
                await_slab(owner, inner, j)

        cosines = entries(cos_row, classes, (size, size))
        sines = entries(sin_row, classes, (size, size))
        rolled[...] = jnp.zeros_like(rolled)

        def first(j, carry):
            masks = bit_masks(held[owner, inner, j], classes)
            cosine, sine = select_tree(masks, cosines), select_tree(masks, sines)
            reals, imags = [], []
            for b in range(beams):
                re = field[j, b * size:(b + 1) * size, 0:size]
                im = field[j, b * size:(b + 1) * size, size:]
                reals.append(re * cosine - im * sine)
                imags.append(re * sine + im * cosine)
            plane = jnp.concatenate([jnp.concatenate(reals, 1), jnp.concatenate(imags, 1)], 0)
            u_high, u_low = split(plane)
            v = jnp.dot(y_band[...], jnp.concatenate([u_high, u_high, u_low], 0), preferred_element_type=F32)
            rows = []
            for b in range(beams):
                cols = [pltpu.roll(v[c * size:(c + 1) * size, b * size:(b + 1) * size], half, 1) for c in range(2)]
                rows.append(jnp.concatenate(cols, 1))
            now = jnp.concatenate(rows, 0)
            shifted(j, rolled[...], now)
            rolled[...] = now
            return carry

        lax.fori_loop(0, tiles, first, 0, unroll=unroll)
        shifted(tiles, rolled[...], jnp.zeros_like(rolled))

        def second(j, carry):
            sides = [high[j], high[j + 1], low[j], low[j + 1], high[j], high[j + 1]]
            field[j] = jnp.dot(jnp.concatenate(sides, 1), z_band[...], preferred_element_type=F32)
            return carry

        @pl.when(step < x_cells - 1)
        def _():
            lax.fori_loop(0, tiles, second, 0, unroll=unroll)

        @pl.when(step == x_cells - 1)
        def _():
            second(tile, 0)

        w = field[tile]
        power = w * w
        power = power[:, :size] + power[:, size:]
        total = power[0:size]
        for b in range(1, beams):
            total = total + power[b * size:(b + 1) * size]
        energy[x] = total
        pl.when(owner != section)(lambda: energy_copy(x).start())
        return carry

    lax.fori_loop(0, x_cells, slice_step, 0)

    blur_y = circulant(taps[4:5, :], size, half)
    blur_z = jnp.concatenate(windows(taps[5:6, :], size), 0)
    label_copy.wait()
    lit = []
    for inner in range(own_x):
        masks = bit_masks(label_held[inner], bright_ref.shape[0])
        lit.append(select_tree(masks, [jnp.full((size, size), bright_ref[k]) for k in range(bright_ref.shape[0])]))

    def received(other, inner):
        return pltpu.make_async_remote_copy(
            src_ref=energy.at[0], dst_ref=gathered.at[other, inner], send_sem=energy_out.at[0],
            recv_sem=energy_in.at[other, inner], device_id={"sect": other}, device_id_type=MESH)

    columns = []
    for inner in range(own_x):
        total = energy[section * own_x + inner]
        for d in range(1, sections):
            received(section_at(d), inner).wait_recv()
            total = total + gathered[section_at(d), inner]
        columns.append(lit[inner] * total)
    blurred = dot3(blur_y, jnp.concatenate(columns, 1))

    top = lax.broadcasted_iota(jnp.int32, (size // 2, size), 1) < half
    turned = []
    for inner in range(own_x):
        block = blurred[:, inner * size:(inner + 1) * size]
        turn = pltpu.roll(block, half, 1)
        turned.append(turn)
        edges[0, inner] = jnp.where(top, turn[:size // 2], block[size // 2:])
        edges[1, inner] = jnp.where(top, block[:size // 2], turn[size // 2:])

    def edge_copy(way):
        return pltpu.make_async_remote_copy(
            src_ref=edges.at[way], dst_ref=edge_in.at[way], send_sem=edge_out.at[way],
            recv_sem=edge_sem.at[way], device_id={"tile": tile_at(1 if way == 0 else tiles - 1)},
            device_id_type=MESH)

    edge_in_ok = (has_before, has_next)
    edge_out_ok = (has_next, has_before)
    for way in range(2):
        pl.when(edge_out_ok[way])(lambda: edge_copy(way).start())
    for way in range(2):
        @pl.when(jnp.logical_not(edge_in_ok[way]))
        def _():
            edge_in[way] = jnp.zeros(edge_in.shape[1:], F32)

        pl.when(edge_in_ok[way])(lambda: edge_copy(way).wait_recv())

    planes = []
    for inner in range(own_x):
        turn = turned[inner]
        before, after = edge_in[0, inner], edge_in[1, inner]
        before = jnp.concatenate([before, pltpu.roll(before, half, 1)], 0)
        after = jnp.concatenate([pltpu.roll(after, half, 1), after], 0)
        planes.append(jnp.concatenate([jnp.where(upper, before, turn), jnp.where(upper, turn, after)], 1))
    image = dot3(jnp.concatenate(planes, 0), blur_z)
    for inner in range(own_x):
        out_ref[inner] = image[inner * size:(inner + 1) * size]

    for way in range(2):
        pl.when(edge_out_ok[way])(lambda: edge_copy(way).wait_send())

    @pl.loop(0, x_cells)
    def _(x):
        pl.when(x // own_x != section)(lambda: energy_copy(x).wait_send())

    @pl.loop(0, tiles)
    def _(j):
        source = held.at[section, own_inner(0), j]
        pl.when(jnp.logical_and(has_next, j <= tile))(lambda: relay_copy(0, j, source).wait_send())
        pl.when(jnp.logical_and(has_before, j >= tile))(lambda: relay_copy(1, j, source).wait_send())

    for n in range(own_x):
        inner = own_inner(n)
        if n > 0:
            @pl.loop(1, tiles)
            def _(d):
                along_copy(inner, d).wait_send()

        @pl.loop(0, tiles)
        def _(j):
            mirror_copy(inner, j, held.at[section, inner, j]).wait_send()
            for kind, owner in ((0, section), (1, mirror)):
                for copy in partner_copies(owner, kind, inner, j, held.at[owner, inner, j]):
                    copy.wait_send()


def on_device(labels, classes, positions, phase_table, brightness, prop_taps, detect_taps):
    own_x, size, _ = labels.shape
    sections, tiles = lax.axis_size("sect"), lax.axis_size("tile")
    x_cells = own_x * sections
    beams = 2 * positions.shape[0] // sections
    vmem, smem = pl.BlockSpec(memory_space=pltpu.VMEM), pl.BlockSpec(memory_space=pltpu.SMEM)
    anywhere = pl.BlockSpec(memory_space=pl.ANY)
    rows = beams * size
    dma = pltpu.SemaphoreType.DMA
    return pl.pallas_call(
        functools.partial(kernel, tiles, sections),
        out_shape=jax.ShapeDtypeStruct((own_x, size, size), F32),
        in_specs=[anywhere, anywhere, smem, smem, smem, vmem, vmem],
        out_specs=vmem,
        scratch_shapes=[
            pltpu.VMEM((sections, own_x, tiles, size, size), jnp.int32),
            pltpu.VMEM((own_x, size, size), jnp.int32),
            pltpu.VMEM((8, 2 * size), F32),
            pltpu.VMEM((2 * size, 6 * size), BF16),
            pltpu.VMEM((12 * size, 2 * size), BF16),
            pltpu.VMEM((tiles, rows, 2 * size), F32),
            pltpu.VMEM((rows, 2 * size), F32),
            pltpu.VMEM((tiles + 1, rows, 2 * size), BF16),
            pltpu.VMEM((tiles + 1, rows, 2 * size), BF16),
            pltpu.VMEM((x_cells, size, size), F32),
            pltpu.VMEM((sections, own_x, size, size), F32),
            pltpu.VMEM((2, own_x, size // 2, size), F32),
            pltpu.VMEM((2, own_x, size // 2, size), F32),
            dma((sections, own_x, tiles)),
            dma((own_x, tiles)),
            dma((2, tiles)),
            dma((own_x, tiles)),
            dma((2, max(sections // 2 - 1, 1), own_x, tiles)),
            dma,
            dma((x_cells,)),
            dma((sections, own_x)),
            dma((2,)),
            dma((2,)),
        ],
        compiler_params=pltpu.CompilerParams(
            vmem_limit_bytes=60 * 1024 * 1024, collective_id=0, has_side_effects=True),
    )(labels, classes, positions, phase_table, brightness, prop_taps, detect_taps)


def solution(mesh):
    in_specs = (
        P(("groups", "sect"), None, "tile"),
        P(("groups", "sect"), None, "tile"),
        P("groups"),
        P(),
        P(),
        P(),
        P(),
    )
    out_specs = P(("groups", "sect"), None, "tile")
    return jax.shard_map(
        on_device, mesh=mesh, in_specs=in_specs, out_specs=out_specs, check_vma=False
    )
```

```python
import functools
import jax
import jax.numpy as jnp
from jax import lax
from jax.experimental import pallas as pl
from jax.experimental.pallas import tpu as pltpu
from jax.sharding import PartitionSpec as P

SHEET_WIDTH = 6.0
AMPLITUDE = 2.0
F32 = jnp.float32
BF16 = jnp.bfloat16
MESH = pl.DeviceIdType.MESH


def split(x):
    high = x.astype(BF16)
    return high, (x - high.astype(F32)).astype(BF16)


def roll_rows(row, size, shift):
    return pltpu.roll(jnp.broadcast_to(row, (size, size)), shift, 1, stride=1, stride_axis=0)


def circulant(row, size, half):
    folded = row[:, :size] + row[:, size:]
    return roll_rows(folded, size, half % size)


def windows(row, size):
    rolled = roll_rows(row[:, :size], size, 0)
    outer = lax.broadcasted_iota(jnp.int32, (size, size), 0)
    inner = lax.broadcasted_iota(jnp.int32, (size, size), 1)
    last = jnp.broadcast_to(row[:, size:size + 1], (size, size))
    first = jnp.where(inner >= outer, rolled, 0.0)
    second = jnp.where(inner < outer, rolled, jnp.where(inner == outer, last, 0.0))
    return first.T, second.T


def select_tree(bits, values):
    while len(values) > 1:
        bit, bits = bits[0], bits[1:]
        values = [jnp.where(bit, values[i + 1], values[i]) for i in range(0, len(values), 2)]
    return values[0]


def bit_masks(indices, count):
    masks, step = [], 1
    while step < count:
        masks.append((indices & step) != 0)
        step *= 2
    return masks


def entries(row, count, shape):
    return [jnp.broadcast_to(row[:, k:k + 1], shape) for k in range(count)]


def dot3(a, b):
    a_high, a_low = split(a)
    b_high, b_low = split(b)
    return jnp.dot(jnp.concatenate([a_high, a_low, a_high], 1), jnp.concatenate([b_high, b_high, b_low], 0),
                   preferred_element_type=F32)


def kernel(tiles, sections, labels_ref, classes_ref, pos_ref, phase_ref, bright_ref, prop_ref, detect_ref, out_ref,
           held, label_held, taps, y_band, z_band, field, rolled, high, low, energy, gathered, edges, edge_in,
           arrived, along, spread, relay, across, beside, label_sem, energy_out, energy_in, edge_out, edge_sem):
    own_x, size = out_ref.shape[0], out_ref.shape[1]
    x_cells = own_x * sections
    count = prop_ref.shape[-1]
    half = count // 2
    section, tile = lax.axis_index("sect"), lax.axis_index("tile")
    per_side = sections // 2
    beams = 2 * pos_ref.shape[0] // sections
    left = section < per_side
    place_in_side = section % per_side
    mirror = (section + per_side) % sections
    partners = [section - place_in_side + (place_in_side + m) % per_side for m in range(1, per_side)]

    def tile_at(d):
        return (tile + d) % tiles

    def section_at(d):
        return (section + d) % sections

    barrier = pltpu.get_barrier_semaphore()

    @pl.loop(1, tiles)
    def _(d):
        pl.semaphore_signal(barrier, inc=1, device_id={"tile": tile_at(d)}, device_id_type=MESH)

    for d in range(1, sections):
        pl.semaphore_signal(barrier, inc=1, device_id={"sect": section_at(d)}, device_id_type=MESH)
    pl.semaphore_wait(barrier, tiles - 1 + sections - 1)

    def within(owner, inner, j, forward):
        x = owner * own_x + inner
        after = jnp.where(forward, x_cells - x, x + 1)
        return jnp.abs(j - tile) <= (half * after + size - 1) // size

    def own_copy(inner):
        return pltpu.make_async_copy(
            classes_ref.at[inner], held.at[section, inner, tile], arrived.at[section, inner, tile])

    def slab_copy(source, owner, inner, j, sem, device):
        return pltpu.make_async_remote_copy(
            src_ref=source, dst_ref=held.at[owner, inner, j], send_sem=sem,
            recv_sem=arrived.at[owner, inner, j], device_id=device, device_id_type=MESH)

    def along_copy(inner, d):
        return slab_copy(classes_ref.at[inner], section, inner, tile, along.at[inner, d], {"tile": tile_at(d)})

    def relay_copy(way, j, source):
        other = tile_at(1 if way == 0 else tiles - 1)
        return slab_copy(source, section, own_inner(0), j, relay.at[way, j], {"tile": other})

    def spread_copy(inner, d):
        return slab_copy(held.at[mirror, inner, tile], mirror, inner, tile, spread.at[inner, d], {"tile": tile_at(d)})

    def mirror_copy(inner, j, source):
        return slab_copy(source, section, inner, j, across.at[inner, j], {"sect": mirror})

    def partner_copies(owner, kind, inner, j, source):
        return [slab_copy(source, owner, inner, j, beside.at[kind, m, inner, j], {"sect": other})
                for m, other in enumerate(partners)]

    def await_slab(owner, inner, j):
        slab_copy(held.at[owner, inner, j], owner, inner, j, across.at[inner, j], {"sect": mirror}).wait_recv()

    first_left, first_right = place_in_side == 0, place_in_side == per_side - 1
    ascending = jnp.where(left, first_left, jnp.logical_not(first_right))
    mirror_ascending = jnp.where(left, jnp.logical_not(first_right), first_left)
    has_next, has_before = tile < tiles - 1, tile > 0

    def own_inner(n):
        return jnp.where(ascending, n, own_x - 1 - n)

    def mirror_inner(n):
        return jnp.where(mirror_ascending, n, own_x - 1 - n)

    for n in range(own_x):
        inner = own_inner(n)
        own_copy(inner).start()
        if n == 0:
            pl.when(has_next)(lambda: relay_copy(0, tile, classes_ref.at[inner]).start())
            pl.when(has_before)(lambda: relay_copy(1, tile, classes_ref.at[inner]).start())
        for copy in partner_copies(section, 0, inner, tile, classes_ref.at[inner]):
            copy.start()
        mirror_copy(inner, tile, classes_ref.at[inner]).start()
    label_copy = pltpu.make_async_copy(labels_ref, label_held, label_sem)
    label_copy.start()

    def send_along():
        for n in range(1, own_x):
            @pl.loop(1, tiles)
            def _(d):
                along_copy(own_inner(n), d).start()

        for n in range(1, own_x):
            inner = mirror_inner(n)
            await_slab(mirror, inner, tile)

            @pl.loop(1, tiles)
            def _(d):
                pl.when(within(mirror, inner, tile_at(d), left))(lambda: spread_copy(inner, d).start())

            for copy in partner_copies(mirror, 1, inner, tile, held.at[mirror, inner, tile]):
                copy.start()

    def serve_own(n):
        inner = own_inner(n)

        def arrival(j, way, onward):
            await_slab(section, inner, j)
            if n == 0:
                pl.when(onward)(lambda: relay_copy(way, j, held.at[section, inner, j]).start())
            for copy in partner_copies(section, 0, inner, j, held.at[section, inner, j]):
                copy.start()
            if n == 0:
                @pl.when(within(section, inner, j, jnp.logical_not(left)))
                def _():
                    mirror_copy(inner, j, held.at[section, inner, j]).start()

        @pl.loop(1, tiles)
        def _(d):
            pl.when(tile - d >= 0)(lambda: arrival(tile - d, 0, has_next))
            pl.when(tile + d < tiles)(lambda: arrival(tile + d, 1, has_before))
            if n == 0:
                pl.when(d == 1)(send_along)

        own_copy(inner).wait()

    def serve_mirror(n):
        inner = mirror_inner(n)

        @pl.loop(0, tiles)
        def _(j):
            wanted = within(mirror, inner, j, left)

            @pl.when(wanted if n == 0 else jnp.logical_and(wanted, j != tile))
            def _():
                await_slab(mirror, inner, j)
                for copy in partner_copies(mirror, 1, inner, j, held.at[mirror, inner, j]):
                    copy.start()

    def energy_copy(x):
        inner = x % own_x
        return pltpu.make_async_remote_copy(
            src_ref=energy.at[x], dst_ref=gathered.at[section, inner], send_sem=energy_out.at[x],
            recv_sem=energy_in.at[section, inner], device_id={"sect": x // own_x}, device_id_type=MESH)

    taps[...] = jnp.zeros_like(taps)
    for axis in range(2):
        for part in range(2):
            n = 2 * axis + part
            taps[n:n + 1, 0:count] = prop_ref[axis, part:part + 1, :]
        taps[4 + axis:5 + axis, 0:count] = detect_ref[axis:axis + 1, :]

    y_re, y_im = (circulant(taps[n:n + 1, :], size, half) for n in (0, 1))
    y_all = jnp.concatenate([jnp.concatenate([y_re, -y_im], 1), jnp.concatenate([y_im, y_re], 1)], 0)
    y_high, y_low = split(y_all)
    y_band[...] = jnp.concatenate([y_high, y_low, y_high], 1)
    z_re, z_im = windows(taps[2:3, :], size), windows(taps[3:4, :], size)
    parts = []
    for side in range(2):
        top = jnp.concatenate([z_re[side], z_im[side]], 1)
        bottom = jnp.concatenate([-z_im[side], z_re[side]], 1)
        parts.append(split(jnp.concatenate([top, bottom], 0)))
    z_band[...] = jnp.concatenate([p[0] for p in parts] * 2 + [p[1] for p in parts], 0)

    classes = phase_ref.shape[0]
    spot = lax.broadcasted_iota(jnp.int32, (8, 128), 1)
    phases = jnp.zeros((8, 128), F32)
    for k in range(classes):
        phases = jnp.where(spot == k, phase_ref[k], phases)
    cos_row, sin_row = jnp.cos(phases)[0:1], jnp.sin(phases)[0:1]
    place = lax.broadcasted_iota(jnp.int32, (size, size), 0).astype(F32)
    for b in range(beams):
        index = place_in_side * beams + b
        offset = (place - pos_ref[index].astype(F32)) / SHEET_WIDTH
        start = AMPLITUDE * jnp.exp(-offset * offset)

        @pl.loop(0, tiles)
        def _(j):
            field[j, b * size:(b + 1) * size, 0:size] = start
            field[j, b * size:(b + 1) * size, size:] = jnp.zeros_like(start)

    lane = lax.broadcasted_iota(jnp.int32, (size, size), 1)
    upper = lane < (size - half)
    unroll = tiles if tiles <= 4 else 1

    def shifted(j, before, now):
        joined = jnp.where(jnp.concatenate([jnp.concatenate([upper] * 2, 1)] * beams, 0), before, now)
        high[j], low[j] = split(joined)

    middle = x_cells // 2

    def slice_step(step, carry):
        x = jnp.where(left, step, x_cells - 1 - step)
        owner, inner = x // own_x, x % own_x
        for n in range(own_x):
            pl.when(step == n)(functools.partial(serve_own, n))
            pl.when(step == (middle - 1 if n == 0 else middle + n if per_side > 1 else middle))(functools.partial(serve_mirror, n))

        @pl.when(owner % per_side != place_in_side)
        def _():
            @pl.loop(0, tiles)
            def _(j):
                wanted = jnp.logical_or(step < middle, within(owner, inner, j, left))
                pl.when(wanted)(lambda: await_slab(owner, inner, j))

        cosines = entries(cos_row, classes, (size, size))
        sines = entries(sin_row, classes, (size, size))
        rolled[...] = jnp.zeros_like(rolled)

        def first(j, carry):
            masks = bit_masks(held[owner, inner, j], classes)
            cosine, sine = select_tree(masks, cosines), select_tree(masks, sines)
            reals, imags = [], []
            for b in range(beams):
                re = field[j, b * size:(b + 1) * size, 0:size]
                im = field[j, b * size:(b + 1) * size, size:]
                reals.append(re * cosine - im * sine)
                imags.append(re * sine + im * cosine)
            plane = jnp.concatenate([jnp.concatenate(reals, 1), jnp.concatenate(imags, 1)], 0)
            u_high, u_low = split(plane)
            v = jnp.dot(y_band[...], jnp.concatenate([u_high, u_high, u_low], 0), preferred_element_type=F32)
            rows = []
            for b in range(beams):
                cols = [pltpu.roll(v[c * size:(c + 1) * size, b * size:(b + 1) * size], half, 1) for c in range(2)]
                rows.append(jnp.concatenate(cols, 1))
            now = jnp.concatenate(rows, 0)
            shifted(j, rolled[...], now)
            rolled[...] = now
            return carry

        lax.fori_loop(0, tiles, first, 0, unroll=unroll)
        shifted(tiles, rolled[...], jnp.zeros_like(rolled))

        def second(j, carry):
            sides = [high[j], high[j + 1], low[j], low[j + 1], high[j], high[j + 1]]
            field[j] = jnp.dot(jnp.concatenate(sides, 1), z_band[...], preferred_element_type=F32)
            return carry

        @pl.when(step < x_cells - 1)
        def _():
            lax.fori_loop(0, tiles, second, 0, unroll=unroll)

        @pl.when(step == x_cells - 1)
        def _():
            second(tile, 0)

        w = field[tile]
        power = w * w
        power = power[:, :size] + power[:, size:]
        total = power[0:size]
        for b in range(1, beams):
            total = total + power[b * size:(b + 1) * size]
        energy[x] = total
        pl.when(owner != section)(lambda: energy_copy(x).start())
        return carry

    lax.fori_loop(0, x_cells, slice_step, 0)

    blur_y = circulant(taps[4:5, :], size, half)
    blur_z = jnp.concatenate(windows(taps[5:6, :], size), 0)
    label_copy.wait()
    lit = []
    for inner in range(own_x):
        masks = bit_masks(label_held[inner], bright_ref.shape[0])
        lit.append(select_tree(masks, [jnp.full((size, size), bright_ref[k]) for k in range(bright_ref.shape[0])]))

    def received(other, inner):
        return pltpu.make_async_remote_copy(
            src_ref=energy.at[0], dst_ref=gathered.at[other, inner], send_sem=energy_out.at[0],
            recv_sem=energy_in.at[other, inner], device_id={"sect": other}, device_id_type=MESH)

    columns = []
    for inner in range(own_x):
        total = energy[section * own_x + inner]
        for d in range(1, sections):
            received(section_at(d), inner).wait_recv()
            total = total + gathered[section_at(d), inner]
        columns.append(lit[inner] * total)
    blurred = dot3(blur_y, jnp.concatenate(columns, 1))

    top = lax.broadcasted_iota(jnp.int32, (size // 2, size), 1) < half
    turned = []
    for inner in range(own_x):
        block = blurred[:, inner * size:(inner + 1) * size]
        turn = pltpu.roll(block, half, 1)
        turned.append(turn)
        edges[0, inner] = jnp.where(top, turn[:size // 2], block[size // 2:])
        edges[1, inner] = jnp.where(top, block[:size // 2], turn[size // 2:])

    def edge_copy(way):
        return pltpu.make_async_remote_copy(
            src_ref=edges.at[way], dst_ref=edge_in.at[way], send_sem=edge_out.at[way],
            recv_sem=edge_sem.at[way], device_id={"tile": tile_at(1 if way == 0 else tiles - 1)},
            device_id_type=MESH)

    edge_in_ok = (has_before, has_next)
    edge_out_ok = (has_next, has_before)
    for way in range(2):
        pl.when(edge_out_ok[way])(lambda: edge_copy(way).start())
    for way in range(2):
        @pl.when(jnp.logical_not(edge_in_ok[way]))
        def _():
            edge_in[way] = jnp.zeros(edge_in.shape[1:], F32)

        pl.when(edge_in_ok[way])(lambda: edge_copy(way).wait_recv())

    planes = []
    for inner in range(own_x):
        turn = turned[inner]
        before, after = edge_in[0, inner], edge_in[1, inner]
        before = jnp.concatenate([before, pltpu.roll(before, half, 1)], 0)
        after = jnp.concatenate([pltpu.roll(after, half, 1), after], 0)
        planes.append(jnp.concatenate([jnp.where(upper, before, turn), jnp.where(upper, turn, after)], 1))
    image = dot3(jnp.concatenate(planes, 0), blur_z)
    for inner in range(own_x):
        out_ref[inner] = image[inner * size:(inner + 1) * size]

    for way in range(2):
        pl.when(edge_out_ok[way])(lambda: edge_copy(way).wait_send())

    @pl.loop(0, x_cells)
    def _(x):
        pl.when(x // own_x != section)(lambda: energy_copy(x).wait_send())

    @pl.loop(0, tiles)
    def _(j):
        source = held.at[section, own_inner(0), j]
        pl.when(jnp.logical_and(has_next, j <= tile))(lambda: relay_copy(0, j, source).wait_send())
        pl.when(jnp.logical_and(has_before, j >= tile))(lambda: relay_copy(1, j, source).wait_send())

    for n in range(own_x):
        inner = own_inner(n)
        if n > 0:
            @pl.loop(1, tiles)
            def _(d):
                along_copy(inner, d).wait_send()

            mirror_copy(inner, tile, classes_ref.at[inner]).wait_send()
            far = mirror_inner(n)

            @pl.loop(1, tiles)
            def _(d):
                pl.when(within(mirror, far, tile_at(d), left))(lambda: spread_copy(far, d).wait_send())

        @pl.loop(0, tiles)
        def _(j):
            if n == 0:
                @pl.when(within(section, inner, j, jnp.logical_not(left)))
                def _():
                    mirror_copy(inner, j, held.at[section, inner, j]).wait_send()

            for copy in partner_copies(section, 0, inner, j, held.at[section, inner, j]):
                copy.wait_send()
            inner_far = mirror_inner(n)

            @pl.when(within(mirror, inner_far, j, left))
            def _():
                for copy in partner_copies(mirror, 1, inner_far, j, held.at[mirror, inner_far, j]):
                    copy.wait_send()


def on_device(labels, classes, positions, phase_table, brightness, prop_taps, detect_taps):
    own_x, size, _ = labels.shape
    sections, tiles = lax.axis_size("sect"), lax.axis_size("tile")
    x_cells = own_x * sections
    beams = 2 * positions.shape[0] // sections
    vmem, smem = pl.BlockSpec(memory_space=pltpu.VMEM), pl.BlockSpec(memory_space=pltpu.SMEM)
    anywhere = pl.BlockSpec(memory_space=pl.ANY)
    rows = beams * size
    dma = pltpu.SemaphoreType.DMA
    return pl.pallas_call(
        functools.partial(kernel, tiles, sections),
        out_shape=jax.ShapeDtypeStruct((own_x, size, size), F32),
        in_specs=[anywhere, anywhere, smem, smem, smem, vmem, vmem],
        out_specs=vmem,
        scratch_shapes=[
            pltpu.VMEM((sections, own_x, tiles, size, size), jnp.int32),
            pltpu.VMEM((own_x, size, size), jnp.int32),
            pltpu.VMEM((8, 2 * size), F32),
            pltpu.VMEM((2 * size, 6 * size), BF16),
            pltpu.VMEM((12 * size, 2 * size), BF16),
            pltpu.VMEM((tiles, rows, 2 * size), F32),
            pltpu.VMEM((rows, 2 * size), F32),
            pltpu.VMEM((tiles + 1, rows, 2 * size), BF16),
            pltpu.VMEM((tiles + 1, rows, 2 * size), BF16),
            pltpu.VMEM((x_cells, size, size), F32),
            pltpu.VMEM((sections, own_x, size, size), F32),
            pltpu.VMEM((2, own_x, size // 2, size), F32),
            pltpu.VMEM((2, own_x, size // 2, size), F32),
            dma((sections, own_x, tiles)),
            dma((own_x, tiles)),
            dma((own_x, tiles)),
            dma((2, tiles)),
            dma((own_x, tiles)),
            dma((2, max(sections // 2 - 1, 1), own_x, tiles)),
            dma,
            dma((x_cells,)),
            dma((sections, own_x)),
            dma((2,)),
            dma((2,)),
        ],
        compiler_params=pltpu.CompilerParams(
            vmem_limit_bytes=60 * 1024 * 1024, collective_id=0, has_side_effects=True),
    )(labels, classes, positions, phase_table, brightness, prop_taps, detect_taps)


def solution(mesh):
    in_specs = (
        P(("groups", "sect"), None, "tile"),
        P(("groups", "sect"), None, "tile"),
        P("groups"),
        P(),
        P(),
        P(),
        P(),
    )
    out_specs = P(("groups", "sect"), None, "tile")
    return jax.shard_map(
        on_device, mesh=mesh, in_specs=in_specs, out_specs=out_specs, check_vma=False
    )
```
